32 devices in a mesh: mem: 4 (over x, core), grid: 8 (over z, y).
Axes of the slice: x: 2, y: 2, z: 4, core: 2. Of those that a mesh axis runs over, the one named last changes fastest.
Arguments:
- obs_ensemble: bfloat16 [256, 32, 256], P('mem', 'grid'), may hold values from -6 to 6
- obs_values: bfloat16 [32, 256], P('grid'), may hold values from -6 to 6
- inverse_error: bfloat16 [32, 256], P('grid'), may hold values from 0.5 to 8
- obs_counts: int32 [32], P('grid'), may hold values from 1 to 256, as said below
- loc_offsets: int32 [32, 4], P('grid'), may hold values from -2 to 2, as said below
- background: bfloat16 [256, 256, 320], P('mem', 'grid'), may hold values from -6 to 6
Outputs:
- analysis: bfloat16 [256, 256, 320], P('mem', 'grid')
The draws below stay inside these ranges and needn't reach their ends.
Inputs may be any that keep to these rules, and one draw needn't show every extreme that they name: `obs_counts`: counts up to about five times their mean; some block in every draw is full. `loc_offsets`: entry 0 of every list is 0 (the block's own observations); the other entries of a list are distinct nonzero offsets.
All inputs are finite; a program needn't handle non-finite values.
Results may differ from the reference program's by a relative error of at most 0.0063.
Values may be sent and summed in bfloat16 or wider, within the bound.
A program may use at most 128 MiB of HBM per device.

```python
import math
import jax
import jax.numpy as jnp
from jax import lax

MEMBERS = 256
VARS = 320
BLOCK_COLS = 8
OBS_SLOTS = 256
REACH = 2
LOC_LEN = 4
NS_STEPS = 6
BLOCKS = 32
COLS = 256


def draw_obs_counts(key, part):
    first, second, third, fourth = jax.random.split(jax.random.fold_in(key, 11), 4)
    light = jax.random.randint(first, (BLOCKS,), 1, OBS_SLOTS // 4 + 1)
    heavy_pick = jax.random.randint(second, (BLOCKS,), 0, 8) == 0
    heavy = jax.random.randint(third, (BLOCKS,), OBS_SLOTS // 2, OBS_SLOTS + 1)
    counts = jnp.where(heavy_pick, heavy, light)
    full_block = jax.random.randint(fourth, (), 0, BLOCKS)
    counts = jnp.where(jnp.arange(BLOCKS) == full_block, OBS_SLOTS, counts)
    return counts.astype(jnp.int32)


def draw_loc_offsets(key, part):
    nonzero = jnp.concatenate([jnp.arange(-REACH, 0), jnp.arange(1, REACH + 1)]).astype(jnp.int32)
    dropped = jax.random.randint(jax.random.fold_in(key, 23), (BLOCKS,), 0, 2 * REACH)
    dropped = jnp.where(jnp.arange(BLOCKS) == 0, REACH, dropped)
    ranks = jnp.arange(2 * REACH - 1)
    kept = jnp.where(ranks[None, :] < dropped[:, None], nonzero[ranks][None, :], nonzero[ranks + 1][None, :])
    own = jnp.zeros((BLOCKS, 1), jnp.int32)
    return jnp.concatenate([own, kept.astype(jnp.int32)], axis=1).astype(jnp.int32)


def block_scale(own_key, extent, cuts, least, largest):
    loudness = 1.0
    for position, blocks in cuts:
        steps = jax.random.uniform(jax.random.fold_in(jax.random.fold_in(own_key, 6), position), (blocks,), jnp.float32, least / len(cuts), largest / len(cuts))
        loudness = loudness * jnp.repeat(jnp.exp(steps), extent[position] // blocks).reshape((-1,) + (1,) * (len(extent) - 1 - position))
    return loudness


def centred(key, dims, scale, bound, cuts=(), kind=jnp.bfloat16):
    loudness = block_scale(key, dims, cuts, -0.22, 0.18) if cuts else 1.0
    array = jax.random.normal(key, dims, jnp.float32) * scale * loudness
    return jnp.minimum(jnp.maximum(array, -bound), bound).astype(kind)


def setup_inputs(seed: int = 0) -> dict:
    keys = jax.random.split(jax.random.key(seed), 7)
    obs_ensemble = centred(keys[0], (MEMBERS, BLOCKS, OBS_SLOTS), 1.0, 6.0, ((0, 4), (1, 8)))
    obs_values = centred(keys[1], (BLOCKS, OBS_SLOTS), 1.0, 6.0, ((0, 8),))
    inverse_error = jnp.clip(jnp.exp(math.log(8.0) - 2.7725887 * jax.random.uniform(keys[2], (BLOCKS, OBS_SLOTS), jnp.float32) ** block_scale(keys[2], (BLOCKS, OBS_SLOTS), ((0, 8),), -0.2, 0.2)), 0.5, 8.0).astype(jnp.bfloat16)
    obs_counts = draw_obs_counts(jax.random.fold_in(keys[6], 71), 0)
    loc_offsets = draw_loc_offsets(jax.random.fold_in(keys[6], 71), 0)
    background = centred(keys[5], (MEMBERS, COLS, VARS), 1.0, 6.0, ((0, 4), (1, 8)))
    return dict(obs_ensemble=obs_ensemble, obs_values=obs_values, inverse_error=inverse_error, obs_counts=obs_counts, loc_offsets=loc_offsets, background=background)


def taper_of(offsets):
    return 1.0 / (1.0 + jnp.abs(offsets).astype(jnp.float32))

def block_weights(members, obs_row, weight_row):
    members_wide = members.astype(jnp.float32)
    obs_mean = lax.optimization_barrier(jnp.mean(members_wide, axis=0))
    scaled = ((members_wide - obs_mean) * weight_row).astype(jnp.bfloat16)
    innovation = (obs_row - obs_mean) * weight_row
    gram = jnp.dot(scaled, scaled.T, preferred_element_type=jnp.float32)
    rhs = jnp.dot(scaled.astype(jnp.float32), innovation, precision=lax.Precision.HIGHEST)
    identity = jnp.eye(MEMBERS, dtype=jnp.float32)
    system = identity + gram / (MEMBERS - 1)
    scale = jnp.sqrt(jnp.sum(system * system))
    upper = system / scale
    lower = identity
    for step in range(NS_STEPS):
        middle = 0.5 * (3.0 * identity - jnp.dot(lower, upper, precision=lax.Precision.HIGHEST))
        upper = jnp.dot(upper, middle, precision=lax.Precision.HIGHEST)
        lower = jnp.dot(middle, lower, precision=lax.Precision.HIGHEST)
    root_inv = lower / jnp.sqrt(scale)
    inner = jnp.dot(root_inv, rhs, precision=lax.Precision.HIGHEST)
    shift = jnp.dot(root_inv, inner, precision=lax.Precision.HIGHEST) / (MEMBERS - 1)
    return (root_inv + shift[:, None]).astype(jnp.bfloat16)

def apply_block(weights, block_state):
    state_wide = block_state.astype(jnp.float32)
    state_mean = lax.optimization_barrier(jnp.mean(state_wide, axis=0))
    perturbation = (state_wide - state_mean).astype(jnp.bfloat16)
    product = lax.dot_general(weights, perturbation, (((0,), (0,)), ((), ())), preferred_element_type=jnp.float32)
    return (state_mean + product).astype(jnp.bfloat16)

def reference(obs_ensemble, obs_values, inverse_error, obs_counts, loc_offsets, background):
    slot_ids = jnp.arange(OBS_SLOTS, dtype=jnp.int32)
    masked_inverse = inverse_error.astype(jnp.float32) * (slot_ids[None, :] < obs_counts[:, None]).astype(jnp.float32)

    def one_block(block):
        offsets = lax.dynamic_index_in_dim(loc_offsets, block, 0, keepdims=False)
        chosen = ((block + offsets) % BLOCKS).astype(jnp.int32)
        members = jnp.take(obs_ensemble, chosen, axis=1).reshape(MEMBERS, LOC_LEN * OBS_SLOTS)
        obs_row = jnp.take(obs_values, chosen, axis=0).astype(jnp.float32).reshape(LOC_LEN * OBS_SLOTS)
        weight_row = (jnp.take(masked_inverse, chosen, axis=0) * taper_of(offsets)[:, None]).reshape(LOC_LEN * OBS_SLOTS)
        weights = block_weights(members, obs_row, weight_row)
        start = (block * BLOCK_COLS).astype(jnp.int32)
        block_state = lax.dynamic_slice_in_dim(background, start, BLOCK_COLS, 1).reshape(MEMBERS, BLOCK_COLS * VARS)
        return apply_block(weights, block_state)
    result = lax.map(one_block, jnp.arange(BLOCKS, dtype=jnp.int32))
    result = result.reshape(BLOCKS, MEMBERS, BLOCK_COLS, VARS).transpose(1, 0, 2, 3)
    return result.reshape(MEMBERS, COLS, VARS)
```

```python
import functools

import jax
import jax.numpy as jnp
from jax import lax
from jax.experimental import pallas as pl
from jax.experimental.pallas import tpu as pltpu
from jax.sharding import PartitionSpec as P

BLOCK_COLS = 8
REACH = 2
NS_STEPS = 6
MESH = pl.DeviceIdType.MESH
HIGHEST = lax.Precision.HIGHEST
NT = (((1,), (1,)), ((), ()))


def dot(a, b):
    return jnp.dot(a, b, precision=HIGHEST, preferred_element_type=jnp.float32)


def kernel(n, grid_n, loc_len, chunks, loc_ref, taper_ref, obs_ref, table_ref, bg_ref, out_ref,
           near, tables, state, upper, lower, sent_w, got_w,
           obs_send, obs_recv, tab_send, tab_recv, own_sem, direct_send, pair_send, pass_send, state_recv,
           w_send, w_recv):
    me = lax.axis_index("mem")
    row = lax.axis_index("grid")
    core = lax.rem(me, 2)
    sibling = me + 1 - 2 * core
    blocks, local, slots = obs_ref.shape
    members = n * local
    width = bg_ref.shape[1]
    step = width // chunks
    rest = n // 2

    def at(mem, shift):
        return {"mem": mem, "grid": lax.rem(row + shift + grid_n, grid_n)}

    barrier = pltpu.get_barrier_semaphore()
    for shift in (0, -1, 1):
        for k in range(0 if shift else 1, n):
            pl.semaphore_signal(barrier, inc=1, device_id=at(lax.rem(me + k, n), shift), device_id_type=MESH)
    own_rows = pl.ds(pl.multiple_of(me * local, local), local)
    own_state = pltpu.make_async_copy(bg_ref, state.at[own_rows], own_sem.at[0])
    own_state.start()
    own_table = pltpu.make_async_copy(table_ref, tables.at[pl.ds(blocks, blocks)], own_sem.at[1])
    own_table.start()
    pl.semaphore_wait(barrier, 3 * n - 1)

    def obs_copy(i, e):
        target = i + e
        return pltpu.make_async_remote_copy(
            src_ref=obs_ref.at[i], dst_ref=near.at[REACH - e, own_rows],
            send_sem=obs_send.at[i, e + REACH], recv_sem=obs_recv.at[REACH - e, me],
            device_id=at(target % n, target // n), device_id_type=MESH)

    def table_copy(side):
        place = 0 if side == 1 else 2 * blocks
        return pltpu.make_async_remote_copy(
            src_ref=table_ref, dst_ref=tables.at[pl.ds(place, blocks)],
            send_sem=tab_send.at[(side + 1) // 2], recv_sem=tab_recv.at[(side + 1) // 2],
            device_id=at(me, side), device_id_type=MESH)

    for side in (-1, 1):
        table_copy(side).start()
    order = [(i, e) for i in range(blocks) for e in range(-REACH, REACH + 1)]
    order.sort(key=lambda p: 0 <= p[0] + p[1] < n)
    for i, e in order:
        target = i + e
        if 0 <= target < n:
            @pl.when(me != target)
            def _():
                obs_copy(i, e).start()

            @pl.when(me == target)
            def _():
                pltpu.make_async_copy(obs_ref.at[i], near.at[REACH - e, own_rows],
                                      obs_recv.at[REACH - e, me]).start()
        else:
            obs_copy(i, e).start()

    def piece(j):
        return pl.ds(j * step, step)

    def direct(k, j):
        peer = lax.rem(me + 2 * k, n)
        return pltpu.make_async_remote_copy(
            src_ref=bg_ref.at[:, piece(j)], dst_ref=state.at[own_rows, piece(j)],
            send_sem=direct_send.at[k, j], recv_sem=state_recv.at[me, j],
            device_id=at(peer, 0), device_id_type=MESH)

    def paired(j):
        return pltpu.make_async_remote_copy(
            src_ref=bg_ref.at[:, piece(j)], dst_ref=state.at[own_rows, piece(j)],
            send_sem=pair_send.at[j], recv_sem=state_recv.at[me, j],
            device_id=at(sibling, 0), device_id_type=MESH)

    def passed(k, j):
        source = lax.rem(me + n - 2 * k, n)
        rows = pl.ds(pl.multiple_of(source * local, local), local)
        return pltpu.make_async_remote_copy(
            src_ref=state.at[rows, piece(j)], dst_ref=state.at[rows, piece(j)],
            send_sem=pass_send.at[k, j], recv_sem=state_recv.at[source, j],
            device_id=at(sibling, 0), device_id_type=MESH)

    def await_state(source, j):
        rows = pl.ds(pl.multiple_of(source * local, local), local)
        ref = state.at[rows, piece(j)]
        pltpu.make_async_copy(ref, ref, state_recv.at[source, j]).wait()

    for j in range(chunks):
        for k in range(1, rest):
            direct(k, j).start()
        paired(j).start()

    own_state.wait()
    own_table.wait()
    for side in (-1, 1):
        table_copy(side).wait_recv()
    for s in range(2 * REACH + 1):
        for source in range(n):
            ref = near.at[s, pl.ds(source * local, local)]
            pltpu.make_async_copy(ref, ref, obs_recv.at[s, source]).wait()

    gram = jnp.zeros((members, members), jnp.float32)
    rhs = jnp.zeros((8, members), jnp.float32)
    for j in range(loc_len):
        offset = loc_ref[me, j]
        wide = near[offset + REACH].astype(jnp.float32)
        table = tables[blocks + me + offset]
        weight = table[1:2] * taper_ref[me, j]
        mean = jnp.sum(wide, axis=0, keepdims=True) * (1.0 / members)
        scaled = ((wide - mean) * weight).astype(jnp.bfloat16)
        innovation = jnp.broadcast_to((table[0:1] - mean) * weight, (8, slots))
        gram = gram + lax.dot_general(scaled, scaled, NT, preferred_element_type=jnp.float32)
        rhs = rhs + lax.dot_general(innovation, scaled.astype(jnp.float32), NT, precision=HIGHEST,
                                    preferred_element_type=jnp.float32)
    across = lax.broadcasted_iota(jnp.int32, (members, members), 0)
    along = lax.broadcasted_iota(jnp.int32, (members, members), 1)
    identity = (across == along).astype(jnp.float32)
    system = identity + gram / (members - 1)
    square = jnp.sum(jnp.sum(system * system, axis=1, keepdims=True), axis=0, keepdims=True)
    scale = jnp.sqrt(square)
    first = system / scale
    middle = 0.5 * (3.0 * identity - first)
    upper[...] = dot(first, middle)
    lower[...] = middle

    def newton(_, carry):
        mid = 1.5 * identity - 0.5 * dot(lower[...], upper[...])
        upper[...] = dot(upper[...], mid)
        lower[...] = dot(mid, lower[...])
        return carry

    lax.fori_loop(0, NS_STEPS - 2, newton, 0)
    middle = 1.5 * identity - 0.5 * dot(lower[...], upper[...])
    root_inv = dot(middle, lower[...]) / jnp.sqrt(scale)
    shift = dot(dot(rhs, root_inv), root_inv) / (members - 1)
    weights = (root_inv + shift[0:1]).astype(jnp.bfloat16).astype(jnp.float32)
    weights = weights - jnp.sum(weights, axis=1, keepdims=True) * (1.0 / members) + 1.0 / members
    high = weights.astype(jnp.bfloat16)
    low = (weights - high.astype(jnp.float32)).astype(jnp.bfloat16)
    sent_w[0] = high
    sent_w[1] = low

    for k in range(1, rest):
        await_state(lax.rem(me + n - 2 * k, n), 0)
        passed(k, 0).start()

    def weight_copy(k):
        peer = lax.rem(me + k, n)
        return pltpu.make_async_remote_copy(
            src_ref=sent_w.at[:, pl.ds(pl.multiple_of(peer * local, local), local)], dst_ref=got_w.at[me],
            send_sem=w_send.at[k], recv_sem=w_recv.at[me], device_id=at(peer, 0), device_id_type=MESH)

    for k in range(1, n):
        weight_copy(k).start()
    own_w = pltpu.make_async_copy(sent_w.at[:, own_rows], got_w.at[me], w_recv.at[me])
    own_w.start()
    for source in range(n):
        pltpu.make_async_copy(got_w.at[source], got_w.at[source], w_recv.at[source]).wait()

    per_block = width // blocks
    for j in range(chunks):
        if j + 1 < chunks:
            for k in range(1, rest):
                await_state(lax.rem(me + n - 2 * k, n), j + 1)
                passed(k, j + 1).start()
        await_state(sibling, j)
        for k in range(1, rest):
            await_state(lax.rem(sibling + n - 2 * k, n), j)
        block = j * step // per_block
        block_state = state[:, piece(j)]
        total = jnp.dot(got_w[block, 0], block_state, preferred_element_type=jnp.float32)
        total = total + jnp.dot(got_w[block, 1], block_state, preferred_element_type=jnp.float32)
        out_ref[:, piece(j)] = total.astype(jnp.bfloat16)

    for i, e in order:
        target = i + e
        if 0 <= target < n:
            @pl.when(me != target)
            def _():
                obs_copy(i, e).wait_send()
        else:
            obs_copy(i, e).wait_send()
    for side in (-1, 1):
        table_copy(side).wait_send()
    for k in range(1, n):
        weight_copy(k).wait_send()
    for j in range(chunks):
        paired(j).wait_send()
        for k in range(1, rest):
            direct(k, j).wait_send()
            passed(k, j).wait_send()


def on_device(n, grid_n, obs_ensemble, obs_values, inverse_error, obs_counts, loc_offsets, background):
    local, blocks, slots = obs_ensemble.shape
    cols, variables = background.shape[1:]
    members = n * local
    loc_len = loc_offsets.shape[1]
    width = cols * variables
    chunks = 2 * blocks
    assert blocks == n and n % 2 == 0
    slot_ids = jnp.arange(slots, dtype=jnp.int32)
    masked = jnp.where(slot_ids[None, :] < obs_counts[:, None], inverse_error.astype(jnp.float32), 0.0)
    table = jnp.stack([obs_values.astype(jnp.float32), masked], axis=1)
    table = jnp.pad(table, ((0, 0), (0, 6), (0, 0)))
    taper = 1.0 / (1.0 + jnp.abs(loc_offsets).astype(jnp.float32))
    dma = pltpu.SemaphoreType.DMA
    smem = pl.BlockSpec(memory_space=pltpu.SMEM)
    vmem = pl.BlockSpec(memory_space=pltpu.VMEM)
    out = pl.pallas_call(
        functools.partial(kernel, n, grid_n, loc_len, chunks),
        out_shape=jax.ShapeDtypeStruct((local, width), jnp.bfloat16),
        in_specs=[smem, smem, vmem, vmem, vmem],
        out_specs=vmem,
        scratch_shapes=[
            pltpu.VMEM((2 * REACH + 1, members, slots), jnp.bfloat16),
            pltpu.VMEM((3 * blocks, 8, slots), jnp.float32),
            pltpu.VMEM((members, width), jnp.bfloat16),
            pltpu.VMEM((members, members), jnp.float32),
            pltpu.VMEM((members, members), jnp.float32),
            pltpu.VMEM((2, members, members), jnp.bfloat16),
            pltpu.VMEM((n, 2, local, members), jnp.bfloat16),
            dma((blocks, 2 * REACH + 1)),
            dma((2 * REACH + 1, n)),
            dma((2,)),
            dma((2,)),
            dma((2,)),
            dma((n // 2, chunks)),
            dma((chunks,)),
            dma((n // 2, chunks)),
            dma((n, chunks)),
            dma((n,)),
            dma((n,)),
        ],
        compiler_params=pltpu.CompilerParams(collective_id=0, has_side_effects=True, vmem_limit_bytes=60 * 2**20),
        name="analysis",
    )(loc_offsets, taper, obs_ensemble.transpose(1, 0, 2), table, background.reshape(local, width))
    return out.reshape(local, cols, variables)


def solution(mesh):
    placed = (
        P("mem", "grid", None),
        P("grid", None),
        P("grid", None),
        P("grid"),
        P("grid", None),
        P("mem", "grid", None),
    )
    body = functools.partial(on_device, mesh.shape["mem"], mesh.shape["grid"])
    return jax.shard_map(body, mesh=mesh, in_specs=placed, out_specs=P("mem", "grid", None), check_vma=False)
```

```python
import functools

import jax
import jax.numpy as jnp
from jax import lax
from jax.experimental import pallas as pl
from jax.experimental.pallas import tpu as pltpu
from jax.sharding import PartitionSpec as P

REACH = 2
NS_STEPS = 6
PIECES = 2
EARLY = 5
MESH = pl.DeviceIdType.MESH
HIGHEST = lax.Precision.HIGHEST
NT = (((1,), (1,)), ((), ()))


def dot(a, b):
    return jnp.dot(a, b, precision=HIGHEST, preferred_element_type=jnp.float32)


def kernel(n, grid_n, loc_ref, counts_ref, obs_ref, values_ref, inverse_ref, bg_ref, out_ref,
           mine, near, own_table, tables, raw, state, upper, lower, sent_w, got_w, result,
           obs_send, obs_pass, obs_recv, tab_send, tab_recv, raw_sem, out_sem, direct_send, pair_send, pass_send,
           state_recv, w_send, w_recv):
    me = lax.axis_index("mem")
    row = lax.axis_index("grid")
    core = lax.rem(me, 2)
    chip = me // 2
    sibling = me + 1 - 2 * core
    rest = n // 2
    local, blocks, slots = obs_ref.shape
    cols, variables = bg_ref.shape[1:]
    members = n * local
    loc_len = loc_ref.shape[1]
    per = cols // blocks
    width = cols * variables
    chunks = PIECES * blocks
    step = width // chunks
    early = chunks * EARLY // 8
    around = 2 + 2 * REACH

    def at(mem, shift):
        return {"mem": mem, "grid": lax.rem(row + shift + grid_n, grid_n)}

    def rows_of(mem):
        return pl.ds(pl.multiple_of(mem * local, local), local)

    barrier = pltpu.get_barrier_semaphore()
    for shift in (0, -1, 1):
        for k in range(0 if shift else 1, n):
            pl.semaphore_signal(barrier, inc=1, device_id=at(lax.rem(me + k, n), shift), device_id_type=MESH)

    def raw_copy(b):
        part = pl.ds(b * per, per)
        return pltpu.make_async_copy(bg_ref.at[:, part], raw.at[:, part], raw_sem.at[b])

    def out_copy(b):
        part = pl.ds(b * per, per)
        return pltpu.make_async_copy(result.at[:, part], out_ref.at[:, part], out_sem.at[b])

    for b in range(blocks):
        raw_copy(b).start()
    mine[...] = jnp.swapaxes(obs_ref[...].astype(jnp.float32), 0, 1).astype(jnp.bfloat16)
    values = values_ref[...].astype(jnp.float32)
    inverse = inverse_ref[...].astype(jnp.float32)
    lane = lax.broadcasted_iota(jnp.int32, (1, slots), 1)
    upmost = lax.broadcasted_iota(jnp.int32, (8, slots), 0) == 0
    for b in range(blocks):
        masked = jnp.where(lane < counts_ref[b], inverse[b : b + 1], 0.0)
        entry = jnp.where(upmost, values[b : b + 1], masked)
        own_table[b] = entry
        tables[blocks + b] = entry
    own_rows = rows_of(me)
    pl.semaphore_wait(barrier, 3 * n - 1)

    def obs_copy(i, q):
        return pltpu.make_async_remote_copy(
            src_ref=mine.at[i], dst_ref=near.at[i - 2 * q + REACH, own_rows],
            send_sem=obs_send.at[i, q + 1], recv_sem=obs_recv.at[i - 2 * q + REACH, me],
            device_id=at(2 * (q % rest) + core, q // rest), device_id_type=MESH)

    def own_obs(i, q):
        u = i - 2 * q + REACH
        return pltpu.make_async_copy(mine.at[i], near.at[u, own_rows], obs_recv.at[u, me])

    def obs_passed(u, k):
        rows = rows_of(2 * k + core)
        return pltpu.make_async_remote_copy(
            src_ref=near.at[u, rows], dst_ref=near.at[u, rows],
            send_sem=obs_pass.at[u, k], recv_sem=obs_recv.at[u, 2 * k + core],
            device_id=at(sibling, 0), device_id_type=MESH)

    def await_obs(u, mem):
        ref = near.at[u, rows_of(mem)]
        pltpu.make_async_copy(ref, ref, obs_recv.at[u, mem]).wait()

    def table_copy(side):
        place = 0 if side == 1 else 2 * blocks
        return pltpu.make_async_remote_copy(
            src_ref=own_table, dst_ref=tables.at[pl.ds(place, blocks)],
            send_sem=tab_send.at[(side + 1) // 2], recv_sem=tab_recv.at[(side + 1) // 2],
            device_id=at(me, side), device_id_type=MESH)

    targets = [(i, q) for i in range(blocks) for q in range(-1, rest + 1) if 0 <= i - 2 * q + REACH < around]
    targets.sort(key=lambda t: 0 <= t[1] < rest)
    for i, q in targets:
        if 0 <= q < rest:
            @pl.when(chip != q)
            def _():
                obs_copy(i, q).start()

            @pl.when(chip == q)
            def _():
                own_obs(i, q).start()
        else:
            obs_copy(i, q).start()
    for side in (-1, 1):
        table_copy(side).start()

    def piece(j):
        return pl.ds(j * step, step)

    def direct(k, j):
        part = state.at[own_rows, piece(j)]
        return pltpu.make_async_remote_copy(
            src_ref=part, dst_ref=part, send_sem=direct_send.at[k, j], recv_sem=state_recv.at[me, j],
            device_id=at(lax.rem(me + 2 * k, n), 0), device_id_type=MESH)

    def paired(j):
        part = state.at[own_rows, piece(j)]
        return pltpu.make_async_remote_copy(
            src_ref=part, dst_ref=part, send_sem=pair_send.at[j], recv_sem=state_recv.at[me, j],
            device_id=at(sibling, 0), device_id_type=MESH)

    def passed(k, j):
        source = lax.rem(me + n - 2 * k, n)
        part = state.at[rows_of(source), piece(j)]
        return pltpu.make_async_remote_copy(
            src_ref=part, dst_ref=part, send_sem=pass_send.at[k, j], recv_sem=state_recv.at[source, j],
            device_id=at(sibling, 0), device_id_type=MESH)

    def await_state(source, j):
        ref = state.at[rows_of(source), piece(j)]
        pltpu.make_async_copy(ref, ref, state_recv.at[source, j]).wait()

    def send_state(j):
        for k in range(1, rest):
            direct(k, j).start()
        paired(j).start()

    for b in range(blocks):
        raw_copy(b).wait()
        whole = raw[:, b * per : (b + 1) * per].astype(jnp.float32)
        by_col = jnp.swapaxes(whole, 0, 1).astype(jnp.bfloat16)
        state[own_rows, b * per * variables : (b + 1) * per * variables] = jnp.concatenate(
            [by_col[c] for c in range(per)], axis=1)
        for j in range(b * PIECES, (b + 1) * PIECES):
            if j < early:
                send_state(j)

    for u in range(around):
        for k in range(rest):
            await_obs(u, 2 * k + core)
            obs_passed(u, k).start()
    for side in (-1, 1):
        table_copy(side).wait_recv()
    for u in range(around):
        for k in range(rest):
            await_obs(u, 2 * k + 1 - core)

    gram = jnp.zeros((members, members), jnp.float32)
    rhs = jnp.zeros((8, members), jnp.float32)
    for j in range(loc_len):
        offset = loc_ref[me, j]
        wide = near[core + offset + REACH].astype(jnp.float32)
        table = tables[blocks + me + offset]
        distance = jnp.abs(jnp.full((1, slots), offset, jnp.int32)).astype(jnp.float32)
        weight = table[1:2] * (1.0 / (1.0 + distance))
        mean = jnp.sum(wide, axis=0, keepdims=True) * (1.0 / members)
        scaled = ((wide - mean) * weight).astype(jnp.bfloat16)
        innovation = jnp.broadcast_to((table[0:1] - mean) * weight, (8, slots))
        gram = gram + lax.dot_general(scaled, scaled, NT, preferred_element_type=jnp.float32)
        rhs = rhs + lax.dot_general(innovation, scaled.astype(jnp.float32), NT, precision=HIGHEST,
                                    preferred_element_type=jnp.float32)
    across = lax.broadcasted_iota(jnp.int32, (members, members), 0)
    along = lax.broadcasted_iota(jnp.int32, (members, members), 1)
    identity = (across == along).astype(jnp.float32)
    system = identity + gram / (members - 1)
    square = jnp.sum(jnp.sum(system * system, axis=1, keepdims=True), axis=0, keepdims=True)
    scale = jnp.sqrt(square)
    first = system / scale
    middle = 0.5 * (3.0 * identity - first)
    upper[...] = dot(first, middle)
    lower[...] = middle

    def newton(_, carry):
        mid = 1.5 * identity - 0.5 * dot(lower[...], upper[...])
        upper[...] = dot(upper[...], mid)
        lower[...] = dot(mid, lower[...])
        return carry

    lax.fori_loop(0, NS_STEPS - 2, newton, 0)
    middle = 1.5 * identity - 0.5 * dot(lower[...], upper[...])
    root_inv = dot(middle, lower[...]) / jnp.sqrt(scale)
    shift = dot(dot(rhs, root_inv), root_inv) / (members - 1)
    sent_w[...] = (root_inv + shift[0:1]).astype(jnp.bfloat16)

    def weight_copy(k):
        peer = lax.rem(me + k, n)
        return pltpu.make_async_remote_copy(
            src_ref=sent_w.at[rows_of(peer)], dst_ref=got_w.at[me],
            send_sem=w_send.at[k], recv_sem=w_recv.at[me], device_id=at(peer, 0), device_id_type=MESH)

    for k in range(1, rest):
        await_state(lax.rem(me + n - 2 * k, n), 0)
        passed(k, 0).start()
    for k in range(1, n):
        weight_copy(k).start()
    pltpu.make_async_copy(sent_w.at[own_rows], got_w.at[me], w_recv.at[me]).start()
    for j in range(early, chunks):
        send_state(j)
    for source in range(n):
        pltpu.make_async_copy(got_w.at[source], got_w.at[source], w_recv.at[source]).wait()

    for b in range(blocks):
        weights = got_w[b].astype(jnp.float32)
        folded = weights - jnp.sum(weights, axis=1, keepdims=True) * (1.0 / members) + 1.0 / members
        high = folded.astype(jnp.bfloat16)
        low = (folded - high.astype(jnp.float32)).astype(jnp.bfloat16)
        for j in range(b * PIECES, (b + 1) * PIECES):
            if j + 1 < chunks:
                for k in range(1, rest):
                    await_state(lax.rem(me + n - 2 * k, n), j + 1)
                    passed(k, j + 1).start()
            await_state(sibling, j)
            for k in range(1, rest):
                await_state(lax.rem(sibling + n - 2 * k, n), j)
        block_state = state[:, b * per * variables : (b + 1) * per * variables]
        total = jnp.dot(high, block_state, preferred_element_type=jnp.float32)
        total = total + jnp.dot(low, block_state, preferred_element_type=jnp.float32)
        by_col = jnp.stack([total[:, c * variables : (c + 1) * variables] for c in range(per)], axis=0)
        result[:, b * per : (b + 1) * per] = jnp.swapaxes(by_col, 0, 1).astype(jnp.bfloat16)
        out_copy(b).start()

    for i, q in targets:
        if 0 <= q < rest:
            @pl.when(chip != q)
            def _():
                obs_copy(i, q).wait_send()
        else:
            obs_copy(i, q).wait_send()
    for u in range(around):
        for k in range(rest):
            obs_passed(u, k).wait_send()
    for side in (-1, 1):
        table_copy(side).wait_send()
    for k in range(1, n):
        weight_copy(k).wait_send()
    for j in range(chunks):
        paired(j).wait_send()
        for k in range(1, rest):
            direct(k, j).wait_send()
            passed(k, j).wait_send()
    for b in range(blocks):
        out_copy(b).wait()


def on_device(n, grid_n, obs_ensemble, obs_values, inverse_error, obs_counts, loc_offsets, background):
    local, blocks, slots = obs_ensemble.shape
    cols, variables = background.shape[1:]
    members = n * local
    width = cols * variables
    chunks = PIECES * blocks
    rest = n // 2
    around = 2 + 2 * REACH
    assert blocks == n and n % 2 == 0
    dma = pltpu.SemaphoreType.DMA
    smem = pl.BlockSpec(memory_space=pltpu.SMEM)
    vmem = pl.BlockSpec(memory_space=pltpu.VMEM)
    whole = pl.BlockSpec(memory_space=pl.ANY)
    return pl.pallas_call(
        functools.partial(kernel, n, grid_n),
        out_shape=jax.ShapeDtypeStruct((local, cols, variables), jnp.bfloat16),
        in_specs=[smem, smem, vmem, vmem, vmem, whole],
        out_specs=whole,
        scratch_shapes=[
            pltpu.VMEM((blocks, local, slots), jnp.bfloat16),
            pltpu.VMEM((around, members, slots), jnp.bfloat16),
            pltpu.VMEM((blocks, 8, slots), jnp.float32),
            pltpu.VMEM((3 * blocks, 8, slots), jnp.float32),
            pltpu.VMEM((local, cols, variables), jnp.bfloat16),
            pltpu.VMEM((members, width), jnp.bfloat16),
            pltpu.VMEM((members, members), jnp.float32),
            pltpu.VMEM((members, members), jnp.float32),
            pltpu.VMEM((members, members), jnp.bfloat16),
            pltpu.VMEM((n, local, members), jnp.bfloat16),
            pltpu.VMEM((local, cols, variables), jnp.bfloat16),
            dma((blocks, rest + 2)),
            dma((around, rest)),
            dma((around, n)),
            dma((2,)),
            dma((2,)),
            dma((blocks,)),
            dma((blocks,)),
            dma((rest, chunks)),
            dma((chunks,)),
            dma((rest, chunks)),
            dma((n, chunks)),
            dma((n,)),
            dma((n,)),
        ],
        compiler_params=pltpu.CompilerParams(collective_id=0, has_side_effects=True, vmem_limit_bytes=60 * 2**20),
        name="analysis",
    )(loc_offsets, obs_counts, obs_ensemble, obs_values, inverse_error, background)


def solution(mesh):
    placed = (
        P("mem", "grid", None),
        P("grid", None),
        P("grid", None),
        P("grid"),
        P("grid", None),
        P("mem", "grid", None),
    )
    body = functools.partial(on_device, mesh.shape["mem"], mesh.shape["grid"])
    return jax.shard_map(body, mesh=mesh, in_specs=placed, out_specs=P("mem", "grid", None), check_vma=False)
```

```python
import functools

import jax
import jax.numpy as jnp
from jax import lax
from jax.experimental import pallas as pl
from jax.experimental.pallas import tpu as pltpu
from jax.sharding import PartitionSpec as P

REACH = 2
NS_STEPS = 6
PIECES = 2
FIRST = 2
EARLY = 5
HUB = 0
MESH = pl.DeviceIdType.MESH
HIGHEST = lax.Precision.HIGHEST
NT = (((1,), (1,)), ((), ()))


def dot(a, b):
    return jnp.dot(a, b, precision=HIGHEST, preferred_element_type=jnp.float32)


def kernel(n, grid_n, loc_ref, counts_ref, obs_ref, values_ref, inverse_ref, bg_ref, result,
           mine, near, own_table, tables, raw, state, upper, lower, sent_w, got_w, group_sem, cross_sem,
           obs_send, obs_pass, obs_recv, tab_send, tab_recv, raw_sem, direct_send, pair_send, pass_send,
           state_recv, w_send, w_recv):
    me = lax.axis_index("mem")
    row = lax.axis_index("grid")
    core = lax.rem(me, 2)
    chip = me // 2
    sibling = me + 1 - 2 * core
    rest = n // 2
    local, blocks, slots = obs_ref.shape
    cols, variables = bg_ref.shape[1:]
    members = n * local
    loc_len = loc_ref.shape[1]
    per = cols // blocks
    width = cols * variables
    chunks = PIECES * blocks
    step = width // chunks
    initial = chunks * FIRST // 8
    early = chunks * EARLY // 8
    around = 2 + 2 * REACH

    def at(mem, shift):
        return {"mem": mem, "grid": lax.rem(row + shift + grid_n, grid_n)}

    def rows_of(mem):
        return pl.ds(pl.multiple_of(mem * local, local), local)

    barrier = pltpu.get_barrier_semaphore()
    for p in range(n):
        if p != HUB:
            @pl.when(me != p)
            def _():
                pl.semaphore_signal(barrier, inc=1, device_id=at(p, 0), device_id_type=MESH)

    def raw_copy(b):
        part = pl.ds(b * per, per)
        return pltpu.make_async_copy(bg_ref.at[:, part], raw.at[:, part], raw_sem.at[b])

    for b in range(blocks):
        raw_copy(b).start()
    mine[...] = jnp.swapaxes(obs_ref[...].astype(jnp.float32), 0, 1).astype(jnp.bfloat16)
    values = values_ref[...].astype(jnp.float32)
    inverse = inverse_ref[...].astype(jnp.float32)
    lane = lax.broadcasted_iota(jnp.int32, (1, slots), 1)
    upmost = lax.broadcasted_iota(jnp.int32, (8, slots), 0) == 0
    for b in range(blocks):
        masked = jnp.where(lane < counts_ref[b], inverse[b : b + 1], 0.0)
        entry = jnp.where(upmost, values[b : b + 1], masked)
        own_table[b] = entry
        tables[blocks + b] = entry
    own_rows = rows_of(me)

    @pl.when(me != HUB)
    def _():
        pl.semaphore_wait(barrier, n - 1)
        pl.semaphore_signal(group_sem, inc=1, device_id=at(HUB, 0), device_id_type=MESH)

    @pl.when(me == HUB)
    def _():
        pl.semaphore_wait(group_sem, n - 1)
        for side in (-1, 1):
            pl.semaphore_signal(barrier, inc=1, device_id=at(HUB, side), device_id_type=MESH)


    def obs_copy(i, q):
        return pltpu.make_async_remote_copy(
            src_ref=mine.at[i], dst_ref=near.at[i - 2 * q + REACH, own_rows],
            send_sem=obs_send.at[i, q + 1], recv_sem=obs_recv.at[i - 2 * q + REACH, me],
            device_id=at(2 * (q % rest) + core, q // rest), device_id_type=MESH)

    def own_obs(i, q):
        u = i - 2 * q + REACH
        return pltpu.make_async_copy(mine.at[i], near.at[u, own_rows], obs_recv.at[u, me])

    def obs_passed(u, k):
        rows = rows_of(2 * k + core)
        return pltpu.make_async_remote_copy(
            src_ref=near.at[u, rows], dst_ref=near.at[u, rows],
            send_sem=obs_pass.at[u, k], recv_sem=obs_recv.at[u, 2 * k + core],
            device_id=at(sibling, 0), device_id_type=MESH)

    def await_obs(u, mem):
        ref = near.at[u, rows_of(mem)]
        pltpu.make_async_copy(ref, ref, obs_recv.at[u, mem]).wait()

    def table_copy(side):
        place = 0 if side == 1 else 2 * blocks
        return pltpu.make_async_remote_copy(
            src_ref=own_table, dst_ref=tables.at[pl.ds(place, blocks)],
            send_sem=tab_send.at[(side + 1) // 2], recv_sem=tab_recv.at[(side + 1) // 2],
            device_id=at(me, side), device_id_type=MESH)

    targets = [(i, q) for i in range(blocks) for q in range(-1, rest + 1) if 0 <= i - 2 * q + REACH < around]
    for i, q in targets:
        if 0 <= q < rest:
            @pl.when(chip != q)
            def _():
                obs_copy(i, q).start()

            @pl.when(chip == q)
            def _():
                own_obs(i, q).start()

    def piece(j):
        return pl.ds(j * step, step)

    def direct(k, j):
        part = state.at[own_rows, piece(j)]
        return pltpu.make_async_remote_copy(
            src_ref=part, dst_ref=part, send_sem=direct_send.at[k, j], recv_sem=state_recv.at[me, j],
            device_id=at(lax.rem(me + 2 * k, n), 0), device_id_type=MESH)

    def paired(j):
        part = state.at[own_rows, piece(j)]
        return pltpu.make_async_remote_copy(
            src_ref=part, dst_ref=part, send_sem=pair_send.at[j], recv_sem=state_recv.at[me, j],
            device_id=at(sibling, 0), device_id_type=MESH)

    def passed(k, j):
        source = lax.rem(me + n - 2 * k, n)
        part = state.at[rows_of(source), piece(j)]
        return pltpu.make_async_remote_copy(
            src_ref=part, dst_ref=part, send_sem=pass_send.at[k, j], recv_sem=state_recv.at[source, j],
            device_id=at(sibling, 0), device_id_type=MESH)

    def await_state(source, j):
        ref = state.at[rows_of(source), piece(j)]
        pltpu.make_async_copy(ref, ref, state_recv.at[source, j]).wait()

    def send_state(j):
        for k in range(1, rest):
            direct(k, j).start()
        paired(j).start()

    for b in range(blocks):
        raw_copy(b).wait()
        state[own_rows, b * per * variables : (b + 1) * per * variables] = (
            raw[:, b * per : (b + 1) * per].reshape(local, per * variables))
        for j in range(b * PIECES, (b + 1) * PIECES):
            if j < initial:
                send_state(j)

    @pl.when(me == HUB)
    def _():
        pl.semaphore_wait(barrier, 2)
        for p in range(n):
            if p != HUB:
                pl.semaphore_signal(cross_sem, inc=1, device_id=at(p, 0), device_id_type=MESH)

    @pl.when(me != HUB)
    def _():
        pl.semaphore_wait(cross_sem, 1)

    for i, q in targets:
        if not 0 <= q < rest:
            obs_copy(i, q).start()
    for side in (-1, 1):
        table_copy(side).start()
    for j in range(initial, early):
        send_state(j)

    for u in range(around):
        for k in range(rest):
            await_obs(u, 2 * k + core)
            obs_passed(u, k).start()
    for side in (-1, 1):
        table_copy(side).wait_recv()
    for u in range(around):
        for k in range(rest):
            await_obs(u, 2 * k + 1 - core)

    gram = jnp.zeros((members, members), jnp.float32)
    rhs = jnp.zeros((8, members), jnp.float32)
    for j in range(loc_len):
        offset = loc_ref[me, j]
        wide = near[core + offset + REACH].astype(jnp.float32)
        table = tables[blocks + me + offset]
        distance = jnp.abs(jnp.full((1, slots), offset, jnp.int32)).astype(jnp.float32)
        weight = table[1:2] * (1.0 / (1.0 + distance))
        mean = jnp.sum(wide, axis=0, keepdims=True) * (1.0 / members)
        scaled = ((wide - mean) * weight).astype(jnp.bfloat16)
        innovation = jnp.broadcast_to((table[0:1] - mean) * weight, (8, slots))
        gram = gram + lax.dot_general(scaled, scaled, NT, preferred_element_type=jnp.float32)
        rhs = rhs + lax.dot_general(innovation, scaled.astype(jnp.float32), NT, precision=HIGHEST,
                                    preferred_element_type=jnp.float32)
    across = lax.broadcasted_iota(jnp.int32, (members, members), 0)
    along = lax.broadcasted_iota(jnp.int32, (members, members), 1)
    identity = (across == along).astype(jnp.float32)
    system = identity + gram / (members - 1)
    square = jnp.sum(jnp.sum(system * system, axis=1, keepdims=True), axis=0, keepdims=True)
    scale = jnp.sqrt(square)
    first = system / scale
    middle = 0.5 * (3.0 * identity - first)
    upper[...] = dot(first, middle)
    lower[...] = middle

    def newton(_, carry):
        mid = 1.5 * identity - 0.5 * dot(lower[...], upper[...])
        upper[...] = dot(upper[...], mid)
        lower[...] = dot(mid, lower[...])
        return carry

    lax.fori_loop(0, NS_STEPS - 2, newton, 0)
    middle = 1.5 * identity - 0.5 * dot(lower[...], upper[...])
    root_inv = dot(middle, lower[...]) / jnp.sqrt(scale)
    shift = dot(dot(rhs, root_inv), root_inv) / (members - 1)
    sent_w[...] = (root_inv + shift[0:1]).astype(jnp.bfloat16)

    def weight_copy(k):
        peer = lax.rem(me + k, n)
        return pltpu.make_async_remote_copy(
            src_ref=sent_w.at[rows_of(peer)], dst_ref=got_w.at[me],
            send_sem=w_send.at[k], recv_sem=w_recv.at[me], device_id=at(peer, 0), device_id_type=MESH)

    for k in range(1, rest):
        await_state(lax.rem(me + n - 2 * k, n), 0)
        passed(k, 0).start()
    for k in range(1, n):
        weight_copy(k).start()
    pltpu.make_async_copy(sent_w.at[own_rows], got_w.at[me], w_recv.at[me]).start()
    for j in range(early, chunks):
        send_state(j)
    for source in range(n):
        pltpu.make_async_copy(got_w.at[source], got_w.at[source], w_recv.at[source]).wait()

    for b in range(blocks):
        weights = got_w[b].astype(jnp.float32)
        folded = weights - jnp.sum(weights, axis=1, keepdims=True) * (1.0 / members) + 1.0 / members
        high = folded.astype(jnp.bfloat16)
        low = (folded - high.astype(jnp.float32)).astype(jnp.bfloat16)
        for j in range(b * PIECES, (b + 1) * PIECES):
            if j + 1 < chunks:
                for k in range(1, rest):
                    await_state(lax.rem(me + n - 2 * k, n), j + 1)
                    passed(k, j + 1).start()
            await_state(sibling, j)
            for k in range(1, rest):
                await_state(lax.rem(sibling + n - 2 * k, n), j)
        block_state = state[:, b * per * variables : (b + 1) * per * variables]
        total = jnp.dot(high, block_state, preferred_element_type=jnp.float32)
        total = total + jnp.dot(low, block_state, preferred_element_type=jnp.float32)
        result[:, b * per * variables : (b + 1) * per * variables] = total.astype(jnp.bfloat16)

    for i, q in targets:
        if 0 <= q < rest:
            @pl.when(chip != q)
            def _():
                obs_copy(i, q).wait_send()
        else:
            obs_copy(i, q).wait_send()
    for u in range(around):
        for k in range(rest):
            obs_passed(u, k).wait_send()
    for side in (-1, 1):
        table_copy(side).wait_send()
    for k in range(1, n):
        weight_copy(k).wait_send()
    for j in range(chunks):
        paired(j).wait_send()
        for k in range(1, rest):
            direct(k, j).wait_send()
            passed(k, j).wait_send()


def spread(blocks, flat_ref, out_ref, columns, sems):
    local, cols, variables = out_ref.shape
    per = cols // blocks
    copies = []
    for b in range(blocks):
        part = pl.ds(b * per, per)
        columns[:, b * per : (b + 1) * per] = (
            flat_ref[:, b * per * variables : (b + 1) * per * variables].reshape(local, per, variables))
        copies.append(pltpu.make_async_copy(columns.at[:, part], out_ref.at[:, part], sems.at[b]))
        copies[-1].start()
    for copy in copies:
        copy.wait()


def on_device(n, grid_n, obs_ensemble, obs_values, inverse_error, obs_counts, loc_offsets, background):
    local, blocks, slots = obs_ensemble.shape
    cols, variables = background.shape[1:]
    members = n * local
    width = cols * variables
    chunks = PIECES * blocks
    rest = n // 2
    around = 2 + 2 * REACH
    assert blocks == n and n % 2 == 0
    dma = pltpu.SemaphoreType.DMA
    smem = pl.BlockSpec(memory_space=pltpu.SMEM)
    vmem = pl.BlockSpec(memory_space=pltpu.VMEM)
    whole = pl.BlockSpec(memory_space=pl.ANY)
    flat = pl.pallas_call(
        functools.partial(kernel, n, grid_n),
        out_shape=pltpu.VMEM((local, width), jnp.bfloat16),
        in_specs=[smem, smem, vmem, vmem, vmem, whole],
        out_specs=vmem,
        scratch_shapes=[
            pltpu.VMEM((blocks, local, slots), jnp.bfloat16),
            pltpu.VMEM((around, members, slots), jnp.bfloat16),
            pltpu.VMEM((blocks, 8, slots), jnp.float32),
            pltpu.VMEM((3 * blocks, 8, slots), jnp.float32),
            pltpu.VMEM((local, cols, variables), jnp.bfloat16),
            pltpu.VMEM((members, width), jnp.bfloat16),
            pltpu.VMEM((members, members), jnp.float32),
            pltpu.VMEM((members, members), jnp.float32),
            pltpu.VMEM((members, members), jnp.bfloat16),
            pltpu.VMEM((n, local, members), jnp.bfloat16),
            pltpu.SemaphoreType.REGULAR,
            pltpu.SemaphoreType.REGULAR,
            dma((blocks, rest + 2)),
            dma((around, rest)),
            dma((around, n)),
            dma((2,)),
            dma((2,)),
            dma((blocks,)),
            dma((rest, chunks)),
            dma((chunks,)),
            dma((rest, chunks)),
            dma((n, chunks)),
            dma((n,)),
            dma((n,)),
        ],
        compiler_params=pltpu.CompilerParams(collective_id=0, has_side_effects=True, vmem_limit_bytes=60 * 2**20),
        name="analysis",
    )(loc_offsets, obs_counts, obs_ensemble, obs_values, inverse_error, background)
    return pl.pallas_call(
        functools.partial(spread, blocks),
        out_shape=jax.ShapeDtypeStruct((local, cols, variables), jnp.bfloat16),
        in_specs=[vmem],
        out_specs=whole,
        scratch_shapes=[pltpu.VMEM((local, cols, variables), jnp.bfloat16), dma((blocks,))],
        compiler_params=pltpu.CompilerParams(vmem_limit_bytes=16 * 2**20),
        name="spread",
    )(flat)


def solution(mesh):
    placed = (
        P("mem", "grid", None),
        P("grid", None),
        P("grid", None),
        P("grid"),
        P("grid", None),
        P("mem", "grid", None),
    )
    body = functools.partial(on_device, mesh.shape["mem"], mesh.shape["grid"])
    return jax.shard_map(body, mesh=mesh, in_specs=placed, out_specs=P("mem", "grid", None), check_vma=False)
```

```python
import functools

import jax
import jax.numpy as jnp
from jax import lax
from jax.experimental import pallas as pl
from jax.experimental.pallas import tpu as pltpu
from jax.sharding import PartitionSpec as P

REACH = 2
NS_STEPS = 6
PIECES = 2
FIRST = 2
EARLY = 6
HUB = 0
MESH = pl.DeviceIdType.MESH
HIGHEST = lax.Precision.HIGHEST
NT = (((1,), (1,)), ((), ()))


def dot(a, b):
    return jnp.dot(a, b, precision=HIGHEST, preferred_element_type=jnp.float32)


def kernel(n, grid_n, loc_ref, counts_ref, obs_ref, values_ref, inverse_ref, bg_ref, result,
           mine, near, own_table, tables, raw, state, upper, lower, sent_w, got_w, group_sem, cross_sem,
           obs_send, obs_pass, obs_recv, tab_send, tab_recv, raw_sem, direct_send, pair_send, pass_send,
           state_recv, w_send, w_recv):
    me = lax.axis_index("mem")
    row = lax.axis_index("grid")
    core = lax.rem(me, 2)
    chip = me // 2
    sibling = me + 1 - 2 * core
    rest = n // 2
    local, blocks, slots = obs_ref.shape
    cols, variables = bg_ref.shape[1:]
    members = n * local
    loc_len = loc_ref.shape[1]
    per = cols // blocks
    width = cols * variables
    chunks = PIECES * blocks
    step = width // chunks
    initial = chunks * FIRST // 8
    early = chunks * EARLY // 8
    around = 2 + 2 * REACH

    def at(mem, shift):
        return {"mem": mem, "grid": lax.rem(row + shift + grid_n, grid_n)}

    def rows_of(mem):
        return pl.ds(pl.multiple_of(mem * local, local), local)

    barrier = pltpu.get_barrier_semaphore()
    for p in range(n):
        if p != HUB:
            @pl.when(me != p)
            def _():
                pl.semaphore_signal(barrier, inc=1, device_id=at(p, 0), device_id_type=MESH)

    def raw_copy(b):
        part = pl.ds(b * per, per)
        return pltpu.make_async_copy(bg_ref.at[:, part], raw.at[:, part], raw_sem.at[b])

    for b in range(blocks):
        raw_copy(b).start()
    mine[...] = jnp.swapaxes(obs_ref[...].astype(jnp.float32), 0, 1).astype(jnp.bfloat16)
    values = values_ref[...].astype(jnp.float32)
    inverse = inverse_ref[...].astype(jnp.float32)
    lane = lax.broadcasted_iota(jnp.int32, (1, slots), 1)
    upmost = lax.broadcasted_iota(jnp.int32, (8, slots), 0) == 0
    for b in range(blocks):
        masked = jnp.where(lane < counts_ref[b], inverse[b : b + 1], 0.0)
        entry = jnp.where(upmost, values[b : b + 1], masked)
        own_table[b] = entry
        tables[blocks + b] = entry
    own_rows = rows_of(me)

    @pl.when(me != HUB)
    def _():
        pl.semaphore_wait(barrier, n - 1)
        pl.semaphore_signal(group_sem, inc=1, device_id=at(HUB, 0), device_id_type=MESH)

    @pl.when(me == HUB)
    def _():
        pl.semaphore_wait(group_sem, n - 1)
        for side in (-1, 1):
            pl.semaphore_signal(barrier, inc=1, device_id=at(HUB, side), device_id_type=MESH)


    def obs_copy(i, q):
        return pltpu.make_async_remote_copy(
            src_ref=mine.at[i], dst_ref=near.at[i - 2 * q + REACH, own_rows],
            send_sem=obs_send.at[i, q + 1], recv_sem=obs_recv.at[i - 2 * q + REACH, me],
            device_id=at(2 * (q % rest) + core, q // rest), device_id_type=MESH)

    def own_obs(i, q):
        u = i - 2 * q + REACH
        return pltpu.make_async_copy(mine.at[i], near.at[u, own_rows], obs_recv.at[u, me])

    def obs_passed(u, k):
        rows = rows_of(2 * k + core)
        return pltpu.make_async_remote_copy(
            src_ref=near.at[u, rows], dst_ref=near.at[u, rows],
            send_sem=obs_pass.at[u, k], recv_sem=obs_recv.at[u, 2 * k + core],
            device_id=at(sibling, 0), device_id_type=MESH)

    def await_obs(u, mem):
        ref = near.at[u, rows_of(mem)]
        pltpu.make_async_copy(ref, ref, obs_recv.at[u, mem]).wait()

    def table_copy(side):
        place = 0 if side == 1 else 2 * blocks
        return pltpu.make_async_remote_copy(
            src_ref=own_table, dst_ref=tables.at[pl.ds(place, blocks)],
            send_sem=tab_send.at[(side + 1) // 2], recv_sem=tab_recv.at[(side + 1) // 2],
            device_id=at(me, side), device_id_type=MESH)

    targets = [(i, q) for i in range(blocks) for q in range(-1, rest + 1) if 0 <= i - 2 * q + REACH < around]
    for i, q in targets:
        if 0 <= q < rest:
            @pl.when(chip != q)
            def _():
                obs_copy(i, q).start()

            @pl.when(chip == q)
            def _():
                own_obs(i, q).start()

    def piece(j):
        return pl.ds(j * step, step)

    def direct(k, j):
        part = state.at[own_rows, piece(j)]
        return pltpu.make_async_remote_copy(
            src_ref=part, dst_ref=part, send_sem=direct_send.at[k, j], recv_sem=state_recv.at[me, j],
            device_id=at(lax.rem(me + 2 * k, n), 0), device_id_type=MESH)

    def paired(j):
        part = state.at[own_rows, piece(j)]
        return pltpu.make_async_remote_copy(
            src_ref=part, dst_ref=part, send_sem=pair_send.at[j], recv_sem=state_recv.at[me, j],
            device_id=at(sibling, 0), device_id_type=MESH)

    def passed(k, j):
        source = lax.rem(me + n - 2 * k, n)
        part = state.at[rows_of(source), piece(j)]
        return pltpu.make_async_remote_copy(
            src_ref=part, dst_ref=part, send_sem=pass_send.at[k, j], recv_sem=state_recv.at[source, j],
            device_id=at(sibling, 0), device_id_type=MESH)

    def await_state(source, j):
        ref = state.at[rows_of(source), piece(j)]
        pltpu.make_async_copy(ref, ref, state_recv.at[source, j]).wait()

    def send_state(j):
        for k in range(1, rest):
            direct(k, j).start()
        paired(j).start()

    for b in range(blocks):
        raw_copy(b).wait()
        state[own_rows, b * per * variables : (b + 1) * per * variables] = (
            raw[:, b * per : (b + 1) * per].reshape(local, per * variables))
        for j in range(b * PIECES, (b + 1) * PIECES):
            if j < initial:
                send_state(j)

    @pl.when(me == HUB)
    def _():
        pl.semaphore_wait(barrier, 2)
        for p in range(n):
            if p != HUB:
                pl.semaphore_signal(cross_sem, inc=1, device_id=at(p, 0), device_id_type=MESH)

    @pl.when(me != HUB)
    def _():
        pl.semaphore_wait(cross_sem, 1)

    for i, q in targets:
        if not 0 <= q < rest:
            obs_copy(i, q).start()
    for side in (-1, 1):
        table_copy(side).start()
    for j in range(initial, early):
        send_state(j)

    for u in range(around):
        for k in range(rest):
            await_obs(u, 2 * k + core)
            obs_passed(u, k).start()
    for side in (-1, 1):
        table_copy(side).wait_recv()
    for u in range(around):
        for k in range(rest):
            await_obs(u, 2 * k + 1 - core)

    gram = jnp.zeros((members, members), jnp.float32)
    rhs = jnp.zeros((8, members), jnp.float32)
    for j in range(loc_len):
        offset = loc_ref[me, j]
        wide = near[core + offset + REACH].astype(jnp.float32)
        table = tables[blocks + me + offset]
        distance = jnp.abs(jnp.full((1, slots), offset, jnp.int32)).astype(jnp.float32)
        weight = table[1:2] * (1.0 / (1.0 + distance))
        mean = jnp.sum(wide, axis=0, keepdims=True) * (1.0 / members)
        scaled = ((wide - mean) * weight).astype(jnp.bfloat16)
        innovation = jnp.broadcast_to((table[0:1] - mean) * weight, (8, slots))
        gram = gram + lax.dot_general(scaled, scaled, NT, preferred_element_type=jnp.float32)
        rhs = rhs + lax.dot_general(innovation, scaled.astype(jnp.float32), NT, precision=HIGHEST,
                                    preferred_element_type=jnp.float32)
    across = lax.broadcasted_iota(jnp.int32, (members, members), 0)
    along = lax.broadcasted_iota(jnp.int32, (members, members), 1)
    identity = (across == along).astype(jnp.float32)
    system = identity + gram / (members - 1)
    square = jnp.sum(jnp.sum(system * system, axis=1, keepdims=True), axis=0, keepdims=True)
    scale = jnp.sqrt(square)
    first = system / scale
    middle = 0.5 * (3.0 * identity - first)
    upper[...] = dot(first, middle)
    lower[...] = middle

    def newton(_, carry):
        mid = 1.5 * identity - 0.5 * dot(lower[...], upper[...])
        upper[...] = dot(upper[...], mid)
        lower[...] = dot(mid, lower[...])
        return carry

    lax.fori_loop(0, NS_STEPS - 2, newton, 0)
    middle = 1.5 * identity - 0.5 * dot(lower[...], upper[...])
    root_inv = dot(middle, lower[...]) / jnp.sqrt(scale)
    shift = dot(dot(rhs, root_inv), root_inv) / (members - 1)
    sent_w[...] = (root_inv + shift[0:1]).astype(jnp.bfloat16)

    def weight_copy(k):
        peer = lax.rem(me + k, n)
        return pltpu.make_async_remote_copy(
            src_ref=sent_w.at[rows_of(peer)], dst_ref=got_w.at[me],
            send_sem=w_send.at[k], recv_sem=w_recv.at[me], device_id=at(peer, 0), device_id_type=MESH)

    for k in range(1, rest):
        await_state(lax.rem(me + n - 2 * k, n), 0)
        passed(k, 0).start()
    for k in range(1, n):
        weight_copy(k).start()
    pltpu.make_async_copy(sent_w.at[own_rows], got_w.at[me], w_recv.at[me]).start()
    for j in range(early, chunks):
        send_state(j)
    for source in range(n):
        pltpu.make_async_copy(got_w.at[source], got_w.at[source], w_recv.at[source]).wait()

    for b in range(blocks):
        weights = got_w[b].astype(jnp.float32)
        folded = weights - jnp.sum(weights, axis=1, keepdims=True) * (1.0 / members) + 1.0 / members
        high = folded.astype(jnp.bfloat16)
        low = (folded - high.astype(jnp.float32)).astype(jnp.bfloat16)
        parts = []
        for j in range(b * PIECES, (b + 1) * PIECES):
            if j + 1 < chunks:
                for k in range(1, rest):
                    await_state(lax.rem(me + n - 2 * k, n), j + 1)
                    passed(k, j + 1).start()
            await_state(sibling, j)
            for k in range(1, rest):
                await_state(lax.rem(sibling + n - 2 * k, n), j)
            piece_state = state[:, j * step : (j + 1) * step]
            total = jnp.dot(high, piece_state, preferred_element_type=jnp.float32)
            total = total + jnp.dot(low, piece_state, preferred_element_type=jnp.float32)
            parts.append(total.astype(jnp.bfloat16))
        result[:, b * per : (b + 1) * per] = jnp.concatenate(parts, axis=1).reshape(local, per, variables)

    for i, q in targets:
        if 0 <= q < rest:
            @pl.when(chip != q)
            def _():
                obs_copy(i, q).wait_send()
        else:
            obs_copy(i, q).wait_send()
    for u in range(around):
        for k in range(rest):
            obs_passed(u, k).wait_send()
    for side in (-1, 1):
        table_copy(side).wait_send()
    for k in range(1, n):
        weight_copy(k).wait_send()
    for j in range(chunks):
        paired(j).wait_send()
        for k in range(1, rest):
            direct(k, j).wait_send()
            passed(k, j).wait_send()


def spread(blocks, held_ref, out_ref, sems):
    per = out_ref.shape[1] // blocks
    parts = [pl.ds(b * per, per) for b in range(blocks)]
    copies = [pltpu.make_async_copy(held_ref.at[:, p], out_ref.at[:, p], sems.at[b]) for b, p in enumerate(parts)]
    for copy in copies:
        copy.start()
    for copy in copies:
        copy.wait()


def on_device(n, grid_n, obs_ensemble, obs_values, inverse_error, obs_counts, loc_offsets, background):
    local, blocks, slots = obs_ensemble.shape
    cols, variables = background.shape[1:]
    members = n * local
    width = cols * variables
    chunks = PIECES * blocks
    rest = n // 2
    around = 2 + 2 * REACH
    assert blocks == n and n % 2 == 0
    dma = pltpu.SemaphoreType.DMA
    smem = pl.BlockSpec(memory_space=pltpu.SMEM)
    vmem = pl.BlockSpec(memory_space=pltpu.VMEM)
    whole = pl.BlockSpec(memory_space=pl.ANY)
    held = pl.pallas_call(
        functools.partial(kernel, n, grid_n),
        out_shape=pltpu.VMEM((local, cols, variables), jnp.bfloat16),
        in_specs=[smem, smem, vmem, vmem, vmem, whole],
        out_specs=vmem,
        scratch_shapes=[
            pltpu.VMEM((blocks, local, slots), jnp.bfloat16),
            pltpu.VMEM((around, members, slots), jnp.bfloat16),
            pltpu.VMEM((blocks, 8, slots), jnp.float32),
            pltpu.VMEM((3 * blocks, 8, slots), jnp.float32),
            pltpu.VMEM((local, cols, variables), jnp.bfloat16),
            pltpu.VMEM((members, width), jnp.bfloat16),
            pltpu.VMEM((members, members), jnp.float32),
            pltpu.VMEM((members, members), jnp.float32),
            pltpu.VMEM((members, members), jnp.bfloat16),
            pltpu.VMEM((n, local, members), jnp.bfloat16),
            pltpu.SemaphoreType.REGULAR,
            pltpu.SemaphoreType.REGULAR,
            dma((blocks, rest + 2)),
            dma((around, rest)),
            dma((around, n)),
            dma((2,)),
            dma((2,)),
            dma((blocks,)),
            dma((rest, chunks)),
            dma((chunks,)),
            dma((rest, chunks)),
            dma((n, chunks)),
            dma((n,)),
            dma((n,)),
        ],
        compiler_params=pltpu.CompilerParams(collective_id=0, has_side_effects=True, vmem_limit_bytes=60 * 2**20),
        name="analysis",
    )(loc_offsets, obs_counts, obs_ensemble, obs_values, inverse_error, background)
    return pl.pallas_call(
        functools.partial(spread, blocks),
        out_shape=jax.ShapeDtypeStruct((local, cols, variables), jnp.bfloat16),
        in_specs=[vmem],
        out_specs=whole,
        scratch_shapes=[dma((blocks,))],
        compiler_params=pltpu.CompilerParams(vmem_limit_bytes=16 * 2**20),
        name="spread",
    )(held)


def solution(mesh):
    placed = (
        P("mem", "grid", None),
        P("grid", None),
        P("grid", None),
        P("grid"),
        P("grid", None),
        P("mem", "grid", None),
    )
    body = functools.partial(on_device, mesh.shape["mem"], mesh.shape["grid"])
    return jax.shard_map(body, mesh=mesh, in_specs=placed, out_specs=P("mem", "grid", None), check_vma=False)
```
